32 devices in a mesh: rep: 4 (over y, x), shard: 8 (over z, core).
Axes of the slice: x: 2, y: 2, z: 4, core: 2. Of those that a mesh axis runs over, the one named last changes fastest.
Arguments:
- tokens: bfloat16 [2, 32, 1024, 768], P(None, ('rep', 'shard')), may hold values from -6 to 6
- cotangent: bfloat16 [2, 32, 1024, 768], P(None, ('rep', 'shard')), may hold values from -6 to 6
- timestep: int32 [2, 32], P(None, ('rep', 'shard')), may hold values from 0 to 1023
- seg_lengths: int32 [2, 32, 12], P(None, ('rep', 'shard')), may hold values from 1 to 128, 768 in all within a row
- attn_gain: bfloat16 [768], P('shard'), may hold values from 0.099609375 to 1.8984375
- w_qkv: bfloat16 [768, 2304], P('shard'), may hold values from -0.3125 to 0.3125
- w_out: bfloat16 [768, 768], P('shard'), may hold values from -1.25 to 1.25
- mlp_gain: bfloat16 [768], P('shard'), may hold values from 0.099609375 to 1.8984375
- w_up: bfloat16 [768, 3072], P('shard'), may hold values from -0.21875 to 0.21875
- b_up: bfloat16 [3072], P('shard'), may hold values from -3 to 3
- w_down: bfloat16 [3072, 768], P('shard'), may hold values from -0.109375 to 0.109375
- b_down: bfloat16 [768], P('shard'), may hold values from -3 to 3
- w_mod: bfloat16 [128, 4608], P(None, 'shard'), may hold values from -0.5 to 0.5
- b_mod: bfloat16 [4608], P('shard'), may hold values from -3 to 3
Outputs:
- output: bfloat16 [2, 32, 1024, 768], P(None, ('rep', 'shard'))
- input_grad: bfloat16 [2, 32, 1024, 768], P(None, ('rep', 'shard'))
- grad_attn_gain: float32 [768], P('shard')
- grad_w_qkv: float32 [768, 2304], P('shard')
- grad_w_out: float32 [768, 768], P('shard')
- grad_mlp_gain: float32 [768], P('shard')
- grad_w_up: float32 [768, 3072], P('shard')
- grad_b_up: float32 [3072], P('shard')
- grad_w_down: float32 [3072, 768], P('shard')
- grad_b_down: float32 [768], P('shard')
- grad_w_mod: float32 [128, 4608], P(None, 'shard')
- grad_b_mod: float32 [4608], P('shard')
The draws below stay inside these ranges and needn't reach their ends.
Inputs may be any that keep to these rules, and one draw needn't show every extreme that they name: `seg_lengths`: the twelve lengths of each tree sum to 768.
All inputs are finite; a program needn't handle non-finite values.
Results may differ from the reference program's by a relative error of at most 0.015.
The reference program's roundings to bfloat16 on the way count: a program that leaves them out, or rounds other values in their place, can miss the bound.
Values may be sent and summed in bfloat16 or wider, within the bound.
A program may use at most 256 MiB of HBM per device.

```python
import math
import jax
import jax.numpy as jnp
import numpy as np
from jax import lax

D = 768
HEADS = 12
HD = 64
FF = 3072
COND = 128
TRUNK = 256
SEG = 64
MB = 2
TSTEPS = 1024
TREES = 32
TLEN = 1024


def with_ends(drawn, rng, least, largest):
    longest = drawn.shape.index(max(drawn.shape))
    spots = []
    for shift in (0, 1):
        where = [jax.random.randint(jax.random.fold_in(rng, axis), (), 0, length) for axis, length in enumerate(drawn.shape)]
        where[longest] = (where[longest] + shift) % drawn.shape[longest]
        spots.append(tuple(where))
    return drawn.at[spots[0]].set(least).at[spots[1]].set(largest)


def steps_of(stream_key, shape, shards, least, largest):
    def one(dim, parts):
        steps = jax.random.uniform(jax.random.fold_in(jax.random.fold_in(stream_key, 6), dim), (parts,), jnp.float32, least / len(shards), largest / len(shards))
        return jnp.repeat(jnp.exp(steps), shape[dim] // parts).reshape((-1,) + (1,) * (len(shape) - dim - 1))

    level = one(*shards[0])
    for cut in shards[1:]:
        level = level * one(*cut)
    return level


def profile(amount, total, reach, lean):
    weights = [(1 << 20) // math.isqrt(grade ** lean) + 1 for grade in range(2, amount + 1)]
    rest, counts = total - reach - (amount - 1), [1] * (amount - 1)
    while rest > 0:
        candidates = [i for i in range(amount - 1) if counts[i] < reach]
        pool, left = sum([weights[i] for i in candidates]), rest
        for i in candidates:
            extra = min(reach - counts[i], max(1, left * weights[i] // pool), rest)
            counts[i] = counts[i] + extra
            rest = rest - extra
    return np.array([reach] + counts)


def ragged_sizes(rng, amount, total, most, lean):
    if amount == 2:
        one = jax.random.randint(rng, (), max(1, total - most), min(most, total - 1) + 1)
        return jnp.stack([one, total - one])
    tallies = jnp.asarray(profile(amount, total, most, lean), jnp.int32)
    twos = (amount - 1) // 2
    giver, receiver = tallies[1:1 + 2 * twos:2], tallies[2:2 + 2 * twos:2]
    margin = jnp.minimum(giver - 1, most - receiver)
    moved = jax.random.randint(jax.random.fold_in(rng, 1), (twos,), 0, 1 << 20) % (margin + 1)
    tallies = tallies.at[1:1 + 2 * twos:2].set(giver - moved).at[2:2 + 2 * twos:2].set(receiver + moved)
    return tallies[jax.random.permutation(jax.random.fold_in(rng, 2), amount)]


def centred(stream_key, dims, width, limit, split=(), held_as=jnp.bfloat16):
    values = width * jax.random.normal(stream_key, dims, jnp.float32)
    if split:
        values = values * steps_of(stream_key, dims, split, -0.22, 0.18)
    return jnp.clip(values, -limit, limit).astype(held_as)


def setup_inputs(seed: int = 0) -> dict:
    arg_keys = jax.random.split(jax.random.key(seed), 15)
    return {
        "tokens": centred(arg_keys[0], (MB, TREES, TLEN, D), 1.0, 6.0, ((1, 32),)),
        "cotangent": centred(arg_keys[1], (MB, TREES, TLEN, D), 1.0, 6.0, ((1, 32),)),
        "timestep": with_ends(jax.random.randint(arg_keys[2], (MB, TREES), 0, TSTEPS), jax.random.fold_in(arg_keys[2], 1), 0, TSTEPS - 1).astype(jnp.int32),
        "seg_lengths": jax.vmap(lambda own: ragged_sizes(own, 12, 12 * SEG, 2 * SEG, 2))(jax.random.split(arg_keys[3], MB * TREES)).reshape((MB, TREES, 12)).astype(jnp.int32),
        "attn_gain": jnp.clip(1.0 + 0.18 * jax.random.normal(arg_keys[4], (D,), jnp.float32), 0.099609375, 1.8984375).astype(jnp.bfloat16),
        "w_qkv": centred(arg_keys[5], (D, 3 * D), (D // 2) ** -0.5, 0.3125, ((0, 8),)),
        "w_out": centred(arg_keys[6], (D, D), (max(D // 32, 8)) ** -0.5, 1.25, ((0, 8),)),
        "mlp_gain": jnp.clip(1.0 + 0.18 * jax.random.normal(arg_keys[7], (D,), jnp.float32), 0.099609375, 1.8984375).astype(jnp.bfloat16),
        "w_up": centred(arg_keys[8], (D, FF), D ** -0.5, 0.21875, ((0, 8),)),
        "b_up": centred(arg_keys[9], (FF,), 0.5, 3.0, ((0, 8),)),
        "w_down": centred(arg_keys[10], (FF, D), FF ** -0.5, 0.109375, ((0, 8),)),
        "b_down": centred(arg_keys[11], (D,), 0.5, 3.0, ((0, 8),)),
        "w_mod": centred(arg_keys[12], (COND, 6 * D), COND ** -0.5, 0.5, ((1, 8),)),
        "b_mod": centred(arg_keys[13], (6 * D,), 0.5, 3.0, ((0, 8),)),
    }


HIGHEST = lax.Precision.HIGHEST

@jax.custom_vjp
def low(v):
    return lax.optimization_barrier(v.astype(jnp.bfloat16)).astype(jnp.float32)

@jax.custom_vjp
def low_back(v):
    return v

def low_keep(v):
    return (low(v), None)

def low_pass(kept, grad):
    return (grad,)

def back_keep(v):
    return (v, None)

def back_low(kept, grad):
    return (low(grad),)
low.defvjp(low_keep, low_pass)
low_back.defvjp(back_keep, back_low)

def time_cond(indices):
    halfway = COND // 2
    frequency = jnp.exp(-math.log(10000.0) * jnp.arange(halfway, dtype=jnp.float32) / halfway)
    angles = indices.astype(jnp.float32)[..., None] * frequency
    return jax.nn.silu(jnp.concatenate([jnp.cos(angles), jnp.sin(angles)], axis=-1))

def segment_ids(length_row):
    bounds = jnp.cumsum(length_row, dtype=jnp.int32)
    places = jnp.arange(TLEN, dtype=jnp.int32)
    offset = places - TRUNK
    inside = lax.optimization_barrier(jnp.sum((offset[:, None] >= bounds[None, :]).astype(jnp.int32), axis=1, dtype=jnp.int32))
    return jnp.where(places < TRUNK, 0, 1 + inside).astype(jnp.int32)

def path_mask(segment):
    parent = jnp.where(segment >= 5, 1 + (segment - 5) // 2, 0)
    keyseg = segment[None, :]
    return (keyseg == 0) | (keyseg == segment[:, None]) | (keyseg == parent[:, None])

def modulated_norm(values, gain_vec, shift_vec, scale_vec):
    center = values - lax.optimization_barrier(jnp.mean(values, axis=-1, keepdims=True))
    spread = lax.optimization_barrier(jnp.mean(center * center, axis=-1, keepdims=True))
    return center * lax.rsqrt(spread + 1e-05) * gain_vec * (1.0 + scale_vec) + shift_vec

def tree_layer(x_full, allowed, cond_row, attn_gain, w_qkv, w_out, mlp_gain, w_up, b_up, w_down, b_down, w_mod, b_mod):
    factor = 1.0 / math.sqrt(HD)
    modulation = jnp.dot(cond_row[None, :], w_mod, precision=HIGHEST)[0] + b_mod
    pieces = [modulation[number * D:(number + 1) * D] for number in range(6)]
    hidden_a = low(modulated_norm(x_full, attn_gain, pieces[0], pieces[1]))
    proj_qkv = low_back(low(jnp.dot(hidden_a, w_qkv, precision=HIGHEST)))
    queries = proj_qkv[:, :D].reshape(TLEN, HEADS, HD)
    keys_all = proj_qkv[:, D:2 * D].reshape(TLEN, HEADS, HD)
    values_all = proj_qkv[:, 2 * D:].reshape(TLEN, HEADS, HD)
    scores = low_back(jnp.einsum('qhd,khd->hqk', queries, keys_all, precision=HIGHEST) * factor)
    scores = jnp.where(allowed[None, :, :], scores, -1e+30)
    maxima = lax.optimization_barrier(jnp.max(scores, axis=-1, keepdims=True))
    exponent = jnp.exp(scores - maxima)
    attn_probs = low(exponent / lax.optimization_barrier(jnp.sum(exponent, axis=-1, keepdims=True)))
    mixed = low_back(low(jnp.einsum('hqk,khd->qhd', attn_probs, values_all, precision=HIGHEST).reshape(TLEN, D)))
    branch = low_back(jnp.dot(mixed, w_out, precision=HIGHEST))
    middle = x_full + pieces[2] * branch
    hidden_m = low(modulated_norm(middle, mlp_gain, pieces[3], pieces[4]))
    upward = low_back(jnp.dot(hidden_m, w_up, precision=HIGHEST) + b_up)
    active = low(jax.nn.gelu(upward, approximate=True))
    downward = low_back(jnp.dot(active, w_down, precision=HIGHEST) + b_down)
    return middle + pieces[5] * downward

def reference(tokens, cotangent, timestep, seg_lengths, attn_gain, w_qkv, w_out, mlp_gain, w_up, b_up, w_down, b_down, w_mod, b_mod):
    params = tuple((weight.astype(jnp.float32) for weight in (attn_gain, w_qkv, w_out, mlp_gain, w_up, b_up, w_down, b_down, w_mod, b_mod)))
    tree_count = MB * TREES
    flat_tokens = tokens.reshape(tree_count, TLEN, D)
    flat_cot = cotangent.reshape(tree_count, TLEN, D)
    conds = low(time_cond(timestep.reshape(tree_count)))
    flat_lengths = seg_lengths.reshape(tree_count, 12)

    def visit(totals, inputs):
        token_row, cot_row, cond_row, length_row = inputs
        allowed = path_mask(segment_ids(length_row))

        def forward(x_full, *weights):
            return tree_layer(x_full, allowed, cond_row, *weights)
        result, pullback = jax.vjp(forward, token_row.astype(jnp.float32), *params)
        gradients = pullback(cot_row.astype(jnp.float32))
        totals = tuple((running + addend for running, addend in zip(totals, gradients[1:])))
        return (totals, (result.astype(jnp.bfloat16), gradients[0].astype(jnp.bfloat16)))
    starting = tuple((jnp.zeros_like(weight) for weight in params))
    totals, (outputs, input_grads) = lax.scan(visit, starting, (flat_tokens, flat_cot, conds, flat_lengths))
    return (outputs.reshape(tokens.shape), input_grads.reshape(tokens.shape), totals[0], totals[1], totals[2], totals[3], totals[4], totals[5], totals[6], totals[7], totals[8], totals[9])
```

```python
import functools
import math

import jax
import jax.numpy as jnp
from jax import lax
from jax.experimental import pallas as pl
from jax.experimental.pallas import tpu as pltpu
from jax.sharding import PartitionSpec as P

D=768; HEADS=12; HD=64; TLEN=1024; TRUNK=256
NT=(((1,),(1,)),((),()))
TN=(((0,),(0,)),((),()))
BIG=-1e30
F32=jnp.float32; BF=jnp.bfloat16

def seg_tables(len_ref, tree, rows, lanes=128):
    pos = lax.broadcasted_iota(jnp.int32,(rows,lanes),0) - TRUNK
    lane = lax.broadcasted_iota(jnp.int32,(rows,lanes),1)
    seg = jnp.where(pos>=0,1,0)
    bound = jnp.int32(0)
    for j in range(12):
        bound = bound + len_ref[tree, j]
        seg = seg + jnp.where((pos>=bound),1,0)
    parent = jnp.where(seg>=5, 1+lax.shift_right_arithmetic(seg-5,1), 0)
    ok = (lane==0)|(lane==seg)|(lane==parent)|(lane>12)
    a = jnp.where(ok, 0.0, BIG).astype(BF)
    b = jnp.where(lane==seg, 1.0, 0.0).astype(BF)
    return a,b

def fwd_kernel(len_ref, q_ref,k_ref,v_ref,o_ref,lse_ref,a_s,kaug,vaug):
    t=pl.program_id(0); hp=pl.program_id(1)
    @pl.when(hp==0)
    def _():
        a,b=seg_tables(len_ref,t,TLEN)
        a_s[...]=a
        kaug[:,128:]=b
        vaug[:,128:]=jnp.ones((TLEN,128),BF)
        lse_ref[...]=jnp.zeros_like(lse_ref)
    kaug[:,:128]=k_ref[...]
    vaug[:,:128]=v_ref[...]
    lane=lax.broadcasted_iota(jnp.int32,(256,128),1)
    for qt in range(4):
        rows=slice(qt*256,qt*256+256)
        nk=256 if qt==0 else TLEN
        q2=q_ref[rows,:]
        outs=[]
        lse_acc=lse_ref[rows,:]
        for h in range(2):
            keep=(lane<64) if h==0 else (lane>=64)
            qh=(jnp.where(keep,q2.astype(F32),0.0)*0.125).astype(BF)
            qa=jnp.concatenate([qh,a_s[rows,:]],axis=1)
            s=lax.dot_general(qa,kaug[:nk,:],NT,preferred_element_type=F32)
            m=jnp.max(s,axis=1,keepdims=True)
            p=jnp.exp(s-m).astype(BF)
            o=jnp.dot(p,vaug[:nk,:],preferred_element_type=F32)
            l=o[:,128:]
            outs.append(o[:,:128]/l)
            lse_acc=jnp.where(lane==2*hp+h, m+jnp.log(l), lse_acc)
        lse_ref[rows,:]=lse_acc
        o_ref[rows,:]=jnp.where(lane<64,outs[0],outs[1]).astype(BF)

def attn_fwd(qkv, lens, trees=2):
    gs=pltpu.PrefetchScalarGridSpec(num_scalar_prefetch=1,grid=(trees,6),
      in_specs=[pl.BlockSpec((TLEN,128),lambda t,h,L:(t,h)),
                pl.BlockSpec((TLEN,128),lambda t,h,L:(t,6+h)),
                pl.BlockSpec((TLEN,128),lambda t,h,L:(t,12+h))],
      out_specs=[pl.BlockSpec((TLEN,128),lambda t,h,L:(t,h)),
                 pl.BlockSpec((TLEN,128),lambda t,h,L:(t,0))],
      scratch_shapes=[pltpu.VMEM((TLEN,128),BF),pltpu.VMEM((TLEN,256),BF),pltpu.VMEM((TLEN,256),BF)])
    return pl.pallas_call(fwd_kernel,grid_spec=gs,
      out_shape=[jax.ShapeDtypeStruct((trees*TLEN,D),BF),jax.ShapeDtypeStruct((trees*TLEN,128),F32)],
      compiler_params=pltpu.CompilerParams(vmem_limit_bytes=60<<20),name="attn_fwd")(lens,qkv,qkv,qkv)


def split3(x):
    hi=x.astype(BF).astype(F32); r=x-hi
    mid=r.astype(BF).astype(F32)
    return hi,mid,r-mid

def bwd_kernel(mode, len_ref,q_ref,k_ref,v_ref,do_ref,o_ref,lse_ref,dq_ref,dk_ref,dv_ref,a_s,b_s,ka,va,dk_acc,dv_acc):
    t=pl.program_id(0); hp=pl.program_id(1)
    lane=lax.broadcasted_iota(jnp.int32,(256,128),1)
    laneT=lax.broadcasted_iota(jnp.int32,(TLEN,128),1)
    @pl.when(hp==0)
    def _():
        a,b=seg_tables(len_ref,t,TLEN)
        hi,mid,lo=split3(lse_ref[...])
        ext=pltpu.roll(hi,16,1)+pltpu.roll(mid,32,1)+pltpu.roll(lo,48,1)
        a_s[...]=(a.astype(F32)-ext).astype(BF)
        b_s[...]=b
        va[:,128:]=jnp.where(laneT<3,1.0,0.0).astype(BF)
    ka[:,:128]=k_ref[...]
    va[:,:128]=v_ref[...]
    kf=k_ref[...].astype(F32)*0.125
    for h in range(2):
        hd=2*hp+h
        on=(laneT==16+hd)|(laneT==32+hd)|(laneT==48+hd)
        ka[:,128:]=jnp.where(on,1.0,b_s[...].astype(F32)).astype(BF)
        keep=(lane<64) if h==0 else (lane>=64)
        keepT=(laneT<64) if h==0 else (laneT>=64)
        kh=jnp.where(keepT,kf,0.0).astype(BF)
        for qt in range(4):
            rows=slice(qt*256,qt*256+256)
            nk=256 if qt==0 else TLEN
            qm=(jnp.where(keep,q_ref[rows,:].astype(F32),0.0)*0.125).astype(BF)
            dof=jnp.where(keep,do_ref[rows,:].astype(F32),0.0)
            dom=dof.astype(BF)
            delta=jnp.sum(dof*o_ref[rows,:].astype(F32),axis=1,keepdims=True)
            dhi,dmid,dlo=split3(delta)
            ext=jnp.where(lane==0,dhi,jnp.where(lane==1,dmid,jnp.where(lane==2,dlo,0.0)))
            doa=jnp.concatenate([dom,(-ext).astype(BF)],axis=1)
            qa=jnp.concatenate([qm,a_s[rows,:]],axis=1)
            st=lax.dot_general(ka[:nk,:],qa,NT,preferred_element_type=F32)
            dpt=lax.dot_general(va[:nk,:],doa,NT,preferred_element_type=F32)
            pt=jnp.exp(st)
            plow=pt.astype(BF)
            ds=(pt*dpt).astype(BF)
            dvp=jnp.dot(plow,dom,preferred_element_type=F32)
            dkp=jnp.dot(ds,qm,preferred_element_type=F32)
            if h==0 and qt==0:
                dk_acc[...]=jnp.zeros_like(dk_acc); dv_acc[...]=jnp.zeros_like(dv_acc)
            dv_acc[:nk,:]+=dvp
            dk_acc[:nk,:]+=dkp
            if mode=="tn":
                dq=lax.dot_general(ds,kh[:nk,:],TN,preferred_element_type=F32)
            else:
                dqt=lax.dot_general(kh[:nk,:],ds,TN,preferred_element_type=F32)
                dq=dqt.T
            if h==0: dq_ref[rows,:]=dq.astype(BF)
            else: dq_ref[rows,:]=jnp.where(lane<64,dq_ref[rows,:].astype(F32),dq).astype(BF)
    dk_ref[...]=dk_acc[...].astype(BF)
    dv_ref[...]=dv_acc[...].astype(BF)

def attn_bwd(qkv, lens, do, o, lse, trees=2, mode="nt"):
    b=lambda off: pl.BlockSpec((TLEN,128),lambda t,h,L:(t,off+h))
    gs=pltpu.PrefetchScalarGridSpec(num_scalar_prefetch=1,grid=(trees,6),
      in_specs=[b(0),b(6),b(12),b(0),b(0),pl.BlockSpec((TLEN,128),lambda t,h,L:(t,0))],
      out_specs=[b(0),b(0),b(0)],
      scratch_shapes=[pltpu.VMEM((TLEN,128),BF),pltpu.VMEM((TLEN,128),BF),pltpu.VMEM((TLEN,256),BF),pltpu.VMEM((TLEN,256),BF),
                      pltpu.VMEM((TLEN,128),F32),pltpu.VMEM((TLEN,128),F32)])
    o1=jax.ShapeDtypeStruct((trees*TLEN,D),BF)
    return pl.pallas_call(functools.partial(bwd_kernel,mode),grid_spec=gs,out_shape=[o1,o1,o1],
      compiler_params=pltpu.CompilerParams(vmem_limit_bytes=60<<20),name="attn_bwd")(lens,qkv,qkv,qkv,do,o,lse)
FF=3072
VL=63<<20
def norm_parts(x):
    mean=jnp.mean(x,axis=1,keepdims=True)
    cen=x-mean
    var=jnp.mean(cen*cen,axis=1,keepdims=True)
    rs=lax.rsqrt(var+1e-5)
    return cen*rs, rs

def qkv_kernel(x_ref,mod_ref,gain_ref,w_ref,ha_ref,o_ref):
    xhat,_=norm_parts(x_ref[...].astype(F32))
    m=mod_ref[0]
    h=(xhat*gain_ref[...]*(1.0+m[1:2])+m[0:1]).astype(BF)
    ha_ref[...]=h
    for j in range(3):
        c=slice(j*768,(j+1)*768)
        o_ref[:,c]=jnp.dot(h,w_ref[:,c],preferred_element_type=F32).astype(BF)

def qkv_fwd(x,mod,gain,w,RB=512):
    n=x.shape[0]; per=TLEN//RB
    return pl.pallas_call(qkv_kernel,grid=(n//RB,),
      in_specs=[pl.BlockSpec((RB,D),lambda i:(i,0)),pl.BlockSpec((1,6,D),lambda i:(i//per,0,0)),
        pl.BlockSpec((1,D),lambda i:(0,0)),pl.BlockSpec((D,3*D),lambda i:(0,0),pipeline_mode=pl.Buffered(1))],
      out_specs=[pl.BlockSpec((RB,D),lambda i:(i,0)),pl.BlockSpec((RB,3*D),lambda i:(i,0))],
      out_shape=[jax.ShapeDtypeStruct((n,D),BF),jax.ShapeDtypeStruct((n,3*D),BF)],
      compiler_params=pltpu.CompilerParams(vmem_limit_bytes=VL),name="qkv_fwd")(x,mod,gain,w)

def pre_kernel(x_ref,c_ref,mx_ref,mod_ref,gain_ref,w_ref,br_ref,hm_ref,dd_ref):
    m=mod_ref[0]
    br=jnp.dot(mx_ref[...],w_ref[...],preferred_element_type=F32)
    br_ref[...]=br
    mid=x_ref[...].astype(F32)+m[2:3]*br
    xhat,_=norm_parts(mid)
    hm_ref[...]=(xhat*gain_ref[...]*(1.0+m[4:5])+m[3:4]).astype(BF)
    dd_ref[...]=(c_ref[...].astype(F32)*m[5:6]).astype(BF)

def mlp_pre(x,c,mixed,mod,gain,w,RB=512):
    n=x.shape[0]; per=TLEN//RB
    rb=pl.BlockSpec((RB,D),lambda i:(i,0))
    return pl.pallas_call(pre_kernel,grid=(n//RB,),
      in_specs=[rb,rb,rb,pl.BlockSpec((1,6,D),lambda i:(i//per,0,0)),
        pl.BlockSpec((1,D),lambda i:(0,0)),pl.BlockSpec((D,D),lambda i:(0,0),pipeline_mode=pl.Buffered(1))],
      out_specs=[rb,rb,rb],
      out_shape=[jax.ShapeDtypeStruct((n,D),F32),jax.ShapeDtypeStruct((n,D),BF),jax.ShapeDtypeStruct((n,D),BF)],
      compiler_params=pltpu.CompilerParams(vmem_limit_bytes=VL),name="mlp_pre")(x,c,mixed,mod,gain,w)

C0=math.sqrt(2/math.pi); C1=0.044715
def core_kernel(RB,hm_ref,dd_ref,wu_ref,bu_ref,wd_ref,dn_ref,dh_ref,gu_ref,gb_ref,gd_ref,act_s,dup_s):
    j=pl.program_id(0)
    n=hm_ref.shape[0]
    @pl.when(j==0)
    def _():
        dn_ref[...]=jnp.zeros_like(dn_ref); dh_ref[...]=jnp.zeros_like(dh_ref)
    gb=jnp.zeros((1,wu_ref.shape[1]),F32)
    for r in range(n//RB):
        rows=slice(r*RB,(r+1)*RB)
        u=jnp.dot(hm_ref[rows,:],wu_ref[...],preferred_element_type=F32)+bu_ref[...]
        u2=u*u
        th=jnp.tanh(C0*u*(1.0+C1*u2))
        cdf=0.5+0.5*th
        act=(u*cdf).astype(BF)
        act_s[rows,:]=act
        gp=cdf+(0.5*C0)*u*(1.0-th*th)*(1.0+(3*C1)*u2)
        da=lax.dot_general(dd_ref[rows,:],wd_ref[...],NT,preferred_element_type=F32)
        dup=(da*gp).astype(BF)
        dup_s[rows,:]=dup
        gb=gb+jnp.sum(dup.astype(F32),axis=0,keepdims=True)
        dn_ref[rows,:]+=jnp.dot(act,wd_ref[...],preferred_element_type=F32)
        dh_ref[rows,:]+=lax.dot_general(dup,wu_ref[...],NT,preferred_element_type=F32)
    gb_ref[...]=gb
    gu_ref[...]=lax.dot_general(hm_ref[...],dup_s[...],TN,preferred_element_type=F32).astype(BF)
    gd_ref[...]=lax.dot_general(act_s[...],dd_ref[...],TN,preferred_element_type=F32).astype(BF)

def mlp_core(hm,dd,wu,bu,wd,C=512,RB=256):
    n=hm.shape[0]
    full=pl.BlockSpec((n,D),lambda j:(0,0),pipeline_mode=pl.Buffered(1))
    return pl.pallas_call(functools.partial(core_kernel,RB),grid=(FF//C,),
      in_specs=[full,full,pl.BlockSpec((D,C),lambda j:(0,j)),pl.BlockSpec((1,C),lambda j:(0,j)),pl.BlockSpec((C,D),lambda j:(j,0))],
      out_specs=[pl.BlockSpec((n,D),lambda j:(0,0)),pl.BlockSpec((n,D),lambda j:(0,0)),
        pl.BlockSpec((D,C),lambda j:(0,j)),pl.BlockSpec((1,C),lambda j:(0,j)),pl.BlockSpec((C,D),lambda j:(j,0))],
      out_shape=[jax.ShapeDtypeStruct((n,D),F32),jax.ShapeDtypeStruct((n,D),F32),jax.ShapeDtypeStruct((D,FF),BF),
        jax.ShapeDtypeStruct((1,FF),F32),jax.ShapeDtypeStruct((FF,D),BF)],
      scratch_shapes=[pltpu.VMEM((n,C),BF),pltpu.VMEM((n,C),BF)],
      compiler_params=pltpu.CompilerParams(vmem_limit_bytes=VL),name="mlp_core")(hm,dd,wu,bu,wd)

def rsum(x): return jnp.sum(x,axis=0,keepdims=True)

def post_kernel(per,x_ref,c_ref,mx_ref,br_ref,dn_ref,dh_ref,dd_ref,mod_ref,gain_ref,bd_ref,w_ref,
                out_ref,dmid_ref,dmx_ref,st_ref,gw_ref,acc):
    i=pl.program_id(0); last=pl.num_programs(0)-1
    m=mod_ref[0]
    c=c_ref[...].astype(F32)
    br=br_ref[...]
    mid=x_ref[...].astype(F32)+m[2:3]*br
    down=dn_ref[...]+bd_ref[...]
    out_ref[...]=(mid+m[5:6]*down).astype(BF)
    xhat,rs=norm_parts(mid)
    dh=dh_ref[...]
    gain=gain_ref[...]
    dhx=dh*xhat
    sdh=rsum(dh); sdhx=rsum(dhx)
    e=dh*((1.0+m[4:5])*gain)
    me=jnp.mean(e,axis=1,keepdims=True)
    mex=jnp.mean(e*xhat,axis=1,keepdims=True)
    dmid=c+(e-me-xhat*mex)*rs
    dmid_ref[...]=dmid
    dbr=(dmid*m[2:3]).astype(BF)
    dmx_ref[...]=lax.dot_general(dbr,w_ref[...],NT,preferred_element_type=F32).astype(BF)
    stats=jnp.concatenate([rsum(dmid*br),sdh,sdhx*gain,rsum(c*down),sdhx*(1.0+m[4:5]),rsum(dd_ref[...].astype(F32)),
                           jnp.zeros((2,D),F32)],axis=0)
    @pl.when(lax.rem(i,per)==0)
    def _(): st_ref[0]=stats
    @pl.when(lax.rem(i,per)!=0)
    def _(): st_ref[0]+=stats
    g=lax.dot_general(mx_ref[...],dbr,TN,preferred_element_type=F32)
    @pl.when(i==0)
    def _(): acc[...]=g
    @pl.when(i!=0)
    def _(): acc[...]+=g
    @pl.when(i==last)
    def _(): gw_ref[...]=acc[...].astype(BF)

def mlp_post(x,c,mixed,br,dn,dh,dd,mod,gain,bd,w,RB=256):
    n=x.shape[0]; per=TLEN//RB
    rb=pl.BlockSpec((RB,D),lambda i:(i,0)); vec=pl.BlockSpec((1,D),lambda i:(0,0))
    return pl.pallas_call(functools.partial(post_kernel,per),grid=(n//RB,),
      in_specs=[rb]*7+[pl.BlockSpec((1,6,D),lambda i:(i//per,0,0)),vec,vec,pl.BlockSpec((D,D),lambda i:(0,0),pipeline_mode=pl.Buffered(1))],
      out_specs=[rb,rb,rb,pl.BlockSpec((1,8,D),lambda i:(i//per,0,0)),pl.BlockSpec((D,D),lambda i:(0,0))],
      out_shape=[jax.ShapeDtypeStruct((n,D),BF),jax.ShapeDtypeStruct((n,D),F32),jax.ShapeDtypeStruct((n,D),BF),
        jax.ShapeDtypeStruct((n//TLEN,8,D),F32),jax.ShapeDtypeStruct((D,D),BF)],
      scratch_shapes=[pltpu.VMEM((D,D),F32)],
      compiler_params=pltpu.CompilerParams(vmem_limit_bytes=VL),name="mlp_post")(x,c,mixed,br,dn,dh,dd,mod,gain,bd,w)

def qkvb_kernel(per,x_ref,ha_ref,dq_ref,dk_ref,dv_ref,dmid_ref,mod_ref,gain_ref,w_ref,dx_ref,st_ref,gw_ref,acc):
    i=pl.program_id(0); last=pl.num_programs(0)-1
    m=mod_ref[0]; gain=gain_ref[...]
    dh=None
    ha=ha_ref[...]
    for j,ref in enumerate((dq_ref,dk_ref,dv_ref)):
        c=slice(j*D,(j+1)*D)
        part=lax.dot_general(ref[...],w_ref[:,c],NT,preferred_element_type=F32)
        dh=part if dh is None else dh+part
        g=lax.dot_general(ha,ref[...],TN,preferred_element_type=F32)
        @pl.when(i==0)
        def _(): acc[:,c]=g
        @pl.when(i!=0)
        def _(): acc[:,c]+=g
    xhat,rs=norm_parts(x_ref[...].astype(F32))
    sdh=rsum(dh); sdhx=rsum(dh*xhat)
    e=dh*((1.0+m[1:2])*gain)
    me=jnp.mean(e,axis=1,keepdims=True)
    mex=jnp.mean(e*xhat,axis=1,keepdims=True)
    dx_ref[...]=(dmid_ref[...]+(e-me-xhat*mex)*rs).astype(BF)
    stats=jnp.concatenate([sdh,sdhx*gain,sdhx*(1.0+m[1:2]),jnp.zeros((5,D),F32)],axis=0)
    @pl.when(lax.rem(i,per)==0)
    def _(): st_ref[0]=stats
    @pl.when(lax.rem(i,per)!=0)
    def _(): st_ref[0]+=stats
    @pl.when(i==last)
    def _(): gw_ref[...]=acc[...].astype(BF)

def qkv_bwd(x,ha,dq,dk,dv,dmid,mod,gain,w,RB=512):
    n=x.shape[0]; per=TLEN//RB
    rb=pl.BlockSpec((RB,D),lambda i:(i,0)); vec=pl.BlockSpec((1,D),lambda i:(0,0))
    return pl.pallas_call(functools.partial(qkvb_kernel,per),grid=(n//RB,),
      in_specs=[rb]*6+[pl.BlockSpec((1,6,D),lambda i:(i//per,0,0)),vec,pl.BlockSpec((D,3*D),lambda i:(0,0),pipeline_mode=pl.Buffered(1))],
      out_specs=[rb,pl.BlockSpec((1,8,D),lambda i:(i//per,0,0)),pl.BlockSpec((D,3*D),lambda i:(0,0))],
      out_shape=[jax.ShapeDtypeStruct((n,D),BF),jax.ShapeDtypeStruct((n//TLEN,8,D),F32),jax.ShapeDtypeStruct((D,3*D),BF)],
      scratch_shapes=[pltpu.VMEM((D,3*D),F32)],
      compiler_params=pltpu.CompilerParams(vmem_limit_bytes=VL),name="qkv_bwd")(x,ha,dq,dk,dv,dmid,mod,gain,w)


HIGHEST = lax.Precision.HIGHEST
COND = 128


def time_cond(indices):
    halfway = COND // 2
    frequency = jnp.exp(-math.log(10000.0) * jnp.arange(halfway, dtype=F32) / halfway)
    angles = indices.astype(F32)[..., None] * frequency
    return jax.nn.silu(jnp.concatenate([jnp.cos(angles), jnp.sin(angles)], axis=-1))


def per_device(shards, tokens, cotangent, timestep, seg_lengths, attn_gain, w_qkv, w_out, mlp_gain,
               w_up, b_up, w_down, b_down, w_mod, b_mod):
    both = ("rep", "shard")
    trees = tokens.shape[0] * tokens.shape[1]
    x = tokens.reshape(trees * TLEN, D)
    c = cotangent.reshape(trees * TLEN, D)
    lens = seg_lengths.reshape(trees, 12)
    gather = lambda w, axis=0: lax.all_gather(w, "shard", axis=axis, tiled=True)
    small = jnp.concatenate([attn_gain, mlp_gain, b_up, b_down, b_mod])
    sizes = [v.shape[0] for v in (attn_gain, mlp_gain, b_up, b_down, b_mod)]
    smalls = gather(small[None])
    vecs, at = [], 0
    for size in sizes:
        vecs.append(smalls[:, at:at + size].reshape(1, -1).astype(F32))
        at += size
    gain_a, gain_m, up_b, down_b, mod_b = vecs
    mod_w = gather(w_mod, 1)
    cond = time_cond(timestep.reshape(trees)).astype(BF)
    mod = (jnp.dot(cond, mod_w, preferred_element_type=F32) + mod_b).reshape(trees, 6, D)
    wq = gather(w_qkv)
    wo = gather(w_out)
    wu = gather(w_up)
    wd = gather(w_down)
    ha, qkv = qkv_fwd(x, mod, gain_a, wq)
    o, lse = attn_fwd(qkv, lens, trees)
    br, hm, dd = mlp_pre(x, c, o, mod, gain_m, wo)
    dn, dh, gu, gb, gd = mlp_core(hm, dd, wu, up_b, wd)
    scatter = lambda g: lax.psum_scatter(g, "shard", scatter_dimension=0, tiled=True)
    finish = lambda g: lax.psum(g, "rep").astype(F32)
    gu = finish(scatter(gu))
    gd = finish(scatter(gd))
    out, dmid, dmx, st, go = mlp_post(x, c, o, br, dn, dh, dd, mod, gain_m, down_b, wo)
    go = finish(scatter(go))
    dq, dk, dv = attn_bwd(qkv, lens, dmx, o, lse, trees)
    dx, st2, gq = qkv_bwd(x, ha, dq, dk, dv, dmid, mod, gain_a, wq)
    gq = finish(scatter(gq))
    dmod = jnp.concatenate([st2[:, 0], st2[:, 1], st[:, 0], st[:, 1], st[:, 2], st[:, 3]], axis=1)
    dmods = lax.all_gather(dmod, both, axis=0, tiled=True)
    conds = lax.all_gather(cond, both, axis=0, tiled=True)
    me = lax.axis_index("shard")
    mine = lambda v: lax.dynamic_slice_in_dim(v, me * (v.shape[-1] // shards), v.shape[-1] // shards, v.ndim - 1)
    dmine = mine(dmods)
    grad_w_mod = jnp.dot(conds.astype(F32).T, dmine, precision=HIGHEST)
    grad_b_mod = jnp.sum(dmine, axis=0)
    sums = lax.psum(jnp.concatenate([st2[:, 2].sum(0), st[:, 4].sum(0), gb[0], st[:, 5].sum(0)]), both)
    ga = mine(sums[:D])
    gm = mine(sums[D:2 * D])
    gbu = mine(sums[2 * D:2 * D + FF])
    gbd = mine(sums[2 * D + FF:])
    return (out.reshape(tokens.shape), dx.reshape(tokens.shape), ga, gq, go, gm, gu, gbu, gd, gbd, grad_w_mod, grad_b_mod)


def solution(mesh):
    rows = P(None, ("rep", "shard"), None, None)
    vec, mat, col = P("shard"), P("shard", None), P(None, "shard")
    in_specs = (rows, rows, P(None, ("rep", "shard")), P(None, ("rep", "shard"), None),
                vec, mat, mat, vec, mat, vec, mat, vec, col, vec)
    out_specs = (rows, rows, vec, mat, mat, vec, mat, vec, mat, vec, col, vec)
    return jax.shard_map(functools.partial(per_device, mesh.shape["shard"]), mesh=mesh,
                         in_specs=in_specs, out_specs=out_specs, check_vma=False)
```
